32 devices in a mesh: ctx: 8 (over z, x), tp: 4 (over y, core).
Axes of the slice: x: 2, y: 2, z: 4, core: 2. Of those that a mesh axis runs over, the one named last changes fastest.
Arguments:
- inputs: bfloat16 [4096, 768], P(('ctx', 'tp')), may hold values from -6 to 6
- positions: int32 [4096], P('ctx'), may hold values from 0 to 3071, as said below
- attn_scale: float32 [768], replicated, may hold values from 0.1 to 1.9
- attn_shift: float32 [768], replicated, may hold values from -4 to 4
- mlp_scale: float32 [768], replicated, may hold values from 0.1 to 1.9
- mlp_shift: float32 [768], replicated, may hold values from -4 to 4
- qkv_weight: bfloat16 [768, 3, 768], P(None, None, 'tp'), may hold values from -0.21875 to 0.21875
- qv_bias: float32 [2, 768], P(None, 'tp'), may hold values from -4 to 4
- dense_weight: bfloat16 [768, 768], P('tp'), may hold values from -1.75 to 1.75
- dense_bias: float32 [768], replicated, may hold values from -5 to 5
- up_weight: bfloat16 [768, 3072], P(None, 'tp'), may hold values from -0.21875 to 0.21875
- up_bias: float32 [3072], P('tp'), may hold values from -4 to 4
- down_weight: bfloat16 [3072, 768], P('tp'), may hold values from -0.109375 to 0.109375
- down_bias: float32 [768], replicated, may hold values from -5 to 5
- cotangent: bfloat16 [4096, 768], P(('ctx', 'tp')), may hold values from -6 to 6
Outputs:
- output: bfloat16 [4096, 768], P(('ctx', 'tp'))
- grad_input: float32 [4096, 768], P(('ctx', 'tp'))
- grad_attn_scale: float32 [768], replicated
- grad_attn_shift: float32 [768], replicated
- grad_mlp_scale: float32 [768], replicated
- grad_mlp_shift: float32 [768], replicated
- grad_qkv: float32 [768, 3, 768], P(None, None, 'tp')
- grad_qv_bias: float32 [2, 768], P(None, 'tp')
- grad_dense: float32 [768, 768], P('tp')
- grad_dense_bias: float32 [768], replicated
- grad_up: float32 [768, 3072], P(None, 'tp')
- grad_up_bias: float32 [3072], P('tp')
- grad_down: float32 [3072, 768], P('tp')
- grad_down_bias: float32 [768], replicated
The draws below stay inside these ranges and needn't reach their ends.
Inputs may be any that keep to these rules, and one draw needn't show every extreme that they name: The sequence holds three documents; positions count from 0 at each document's first token and rise by one along it; the second document has 3072 tokens and starts at a token between 1 and 1023.
All inputs are finite; a program needn't handle non-finite values.
Results may differ from the reference program's by a relative error of at most 0.025.
Values may be sent and summed in bfloat16 or wider, within the bound.
A program may use at most 128 MiB of HBM per device.

```python
import jax
import jax.numpy as jnp
from jax import lax

D = 768
H = 12
HD = 64
ROT = 16
FF = 3072
TOKENS = 4096


def draw_positions(key, part):
    start_draw = jax.random.fold_in(key, 17)
    long_start = jax.random.randint(start_draw, (), 1, TOKENS // 4)
    long_end = long_start + 3 * TOKENS // 4
    places = jnp.arange(TOKENS, dtype=jnp.int32)
    doc_start = jnp.where(places >= long_end, long_end, jnp.where(places >= long_start, long_start, 0))
    return (places - doc_start).astype(jnp.int32)


def shard_levels(own_key, shape, shards, low, largest):
    loudness = 1.0
    for position, shards_of in shards:
        steps = jax.random.uniform(jax.random.fold_in(jax.random.fold_in(own_key, 6), position), (shards_of,), jnp.float32, low / len(shards), largest / len(shards))
        loudness = loudness * jnp.repeat(jnp.exp(steps), shape[position] // shards_of).reshape((-1,) + (1,) * (len(shape) - 1 - position))
    return loudness


def scatter_about(own_key, shape, spread, bound, split=(), held_as=jnp.bfloat16):
    drawn = spread * jax.random.normal(own_key, shape, jnp.float32)
    if split:
        drawn = drawn * shard_levels(own_key, shape, split, -0.22, 0.18)
    return jnp.clip(drawn, -bound, bound).astype(held_as)


def setup_inputs(seed: int = 0) -> dict:
    arg_keys = jax.random.split(jax.random.key(seed), 16)
    inputs = scatter_about(arg_keys[0], (TOKENS, D), 1.0, 6.0, ((0, 32),))
    positions = draw_positions(jax.random.fold_in(arg_keys[15], 71), 0)
    attn_scale = jnp.clip(1.0 + 0.18 * jax.random.normal(arg_keys[2], (D,), jnp.float32), 0.1, 1.9)
    attn_shift = scatter_about(arg_keys[3], (D,), 1.0, 4.0, (), jnp.float32)
    mlp_scale = jnp.clip(1.0 + 0.18 * jax.random.normal(arg_keys[4], (D,), jnp.float32), 0.1, 1.9)
    mlp_shift = scatter_about(arg_keys[5], (D,), 1.0, 4.0, (), jnp.float32)
    qkv_weight = scatter_about(arg_keys[6], (D, 3, H * HD), D ** -0.5, 0.21875, ((2, 4),))
    qv_bias = scatter_about(arg_keys[7], (2, H * HD), 1.0, 4.0, ((1, 4),), jnp.float32)
    dense_weight = scatter_about(arg_keys[8], (H * HD, D), (H * HD // 64) ** -0.5, 1.75, ((0, 4),))
    dense_bias = scatter_about(arg_keys[9], (D,), 1.25, 5.0, (), jnp.float32)
    up_weight = scatter_about(arg_keys[10], (D, FF), D ** -0.5, 0.21875, ((1, 4),))
    up_bias = scatter_about(arg_keys[11], (FF,), 1.0, 4.0, ((0, 4),), jnp.float32)
    down_weight = scatter_about(arg_keys[12], (FF, D), FF ** -0.5, 0.109375, ((0, 4),))
    down_bias = scatter_about(arg_keys[13], (D,), 1.25, 5.0, (), jnp.float32)
    cotangent = scatter_about(arg_keys[14], (TOKENS, D), 1.0, 6.0, ((0, 32),))
    return {"inputs": inputs, "positions": positions, "attn_scale": attn_scale, "attn_shift": attn_shift, "mlp_scale": mlp_scale, "mlp_shift": mlp_shift, "qkv_weight": qkv_weight, "qv_bias": qv_bias, "dense_weight": dense_weight, "dense_bias": dense_bias, "up_weight": up_weight, "up_bias": up_bias, "down_weight": down_weight, "down_bias": down_bias, "cotangent": cotangent}


norm_eps = 1e-05

def layer_norm(values, scale, shift):
    mean_value = lax.optimization_barrier(jnp.mean(values, axis=-1, keepdims=True))
    centred = values - mean_value
    variance = lax.optimization_barrier(jnp.mean(centred * centred, axis=-1, keepdims=True))
    inv_std = lax.rsqrt(variance + norm_eps)
    normal_part = centred * inv_std
    return (normal_part * scale + shift, normal_part, inv_std)

def norm_backward(grad_normed, normal_part, inv_std, scale):
    grad_hat = grad_normed * scale
    mean_grad = lax.optimization_barrier(jnp.mean(grad_hat, axis=-1, keepdims=True))
    mean_mixed = lax.optimization_barrier(jnp.mean(grad_hat * normal_part, axis=-1, keepdims=True))
    return inv_std * (grad_hat - mean_grad - normal_part * mean_mixed)

def rotary_tables(positions):
    freqs = 10000.0 ** (-jnp.arange(0, ROT, 2).astype(jnp.float32) / ROT)
    angles = positions.astype(jnp.float32)[:, None] * freqs[None, :]
    angles = jnp.concatenate([angles, angles], axis=1)
    return (jnp.cos(angles), jnp.sin(angles))

def rotate(tensor, cosines, sines):
    part = tensor[..., :ROT]
    half = ROT // 2
    turned = jnp.concatenate([-part[..., half:], part[..., :half]], axis=-1)
    spun = part * cosines[:, None, :] + turned * sines[:, None, :]
    return jnp.concatenate([spun, tensor[..., ROT:]], axis=-1)

def gelu_grad(pre_act):
    cumulative = 0.5 * (1.0 + jax.scipy.special.erf(pre_act * 0.7071067811865476))
    density = jnp.exp(-0.5 * pre_act * pre_act) * 0.3989422804014327
    return cumulative + pre_act * density

def reference(inputs, positions, attn_scale, attn_shift, mlp_scale, mlp_shift, qkv_weight, qv_bias, dense_weight, dense_bias, up_weight, up_bias, down_weight, down_bias, cotangent):
    width = H * HD
    score_scale = HD ** (-0.5)
    resid = inputs.astype(jnp.float32)
    normed_one, hat_one, std_one = layer_norm(resid, attn_scale, attn_shift)
    normed_two, hat_two, std_two = layer_norm(resid, mlp_scale, mlp_shift)
    attn_in = normed_one.astype(jnp.bfloat16)
    mlp_in = normed_two.astype(jnp.bfloat16)
    proj = jnp.dot(attn_in, qkv_weight.reshape(D, 3 * width), preferred_element_type=jnp.float32)
    proj = proj.reshape(TOKENS, 3, H, HD)
    cosines, sines = rotary_tables(positions)
    queries = rotate(proj[:, 0] + qv_bias[0].reshape(H, HD), cosines, sines).astype(jnp.bfloat16)
    keys_rot = rotate(proj[:, 1], cosines, sines).astype(jnp.bfloat16)
    values = (proj[:, 2] + qv_bias[1].reshape(H, HD)).astype(jnp.bfloat16)
    places = jnp.arange(TOKENS, dtype=jnp.int32)
    first_key = (places - positions).astype(jnp.int32)
    block = min(256, TOKENS)
    count = TOKENS // block
    key_float = keys_rot.astype(jnp.float32)
    value_float = values.astype(jnp.float32)

    def block_scores(number):
        start_row = (number * block).astype(jnp.int32)
        query_block = lax.dynamic_slice_in_dim(queries, start_row, block, 0).astype(jnp.float32)
        query_pos = start_row + jnp.arange(block, dtype=jnp.int32)
        first_block = lax.dynamic_slice_in_dim(first_key, start_row, block, 0)
        visible = (places[None, :] <= query_pos[:, None]) & (places[None, :] >= first_block[:, None])
        scores = jnp.einsum('qhd,khd->hqk', query_block, key_float) * score_scale
        return (start_row, query_block, visible, scores)

    def forward_block(number):
        start_row, query_block, visible, scores = block_scores(number)
        scores = jnp.where(visible[None], scores, -1e+30)
        row_max = lax.optimization_barrier(jnp.max(scores, axis=-1))
        weights = jnp.where(visible[None], jnp.exp(scores - row_max[..., None]), 0.0)
        row_sum = lax.optimization_barrier(jnp.sum(weights, axis=-1))
        low = lax.optimization_barrier(weights.astype(jnp.bfloat16)).astype(jnp.float32)
        summed = jnp.einsum('hqk,khd->qhd', low, value_float)
        attended = summed / jnp.transpose(row_sum)[:, :, None]
        return (attended.astype(jnp.bfloat16), row_max + jnp.log(row_sum))
    attended, log_total = lax.map(forward_block, jnp.arange(count))
    attended = attended.reshape(TOKENS, H, HD)
    attended_flat = attended.reshape(TOKENS, width)
    attn_part = jnp.dot(attended_flat, dense_weight, preferred_element_type=jnp.float32)
    pre_act = jnp.dot(mlp_in, up_weight, preferred_element_type=jnp.float32) + up_bias
    activation = jax.nn.gelu(pre_act, approximate=False).astype(jnp.bfloat16)
    mlp_part = jnp.dot(activation, down_weight, preferred_element_type=jnp.float32)
    output = (resid + (attn_part + mlp_part) + dense_bias + down_bias).astype(jnp.bfloat16)
    grad_out = cotangent.astype(jnp.float32)
    bias_grad = lax.optimization_barrier(jnp.sum(grad_out, axis=0))
    grad_down = jnp.dot(activation.T, cotangent, preferred_element_type=jnp.float32)
    grad_act = jnp.dot(cotangent, down_weight.T, preferred_element_type=jnp.float32)
    grad_pre = grad_act * gelu_grad(pre_act)
    grad_up_bias = lax.optimization_barrier(jnp.sum(grad_pre, axis=0))
    grad_pre_low = grad_pre.astype(jnp.bfloat16)
    grad_up = jnp.dot(mlp_in.T, grad_pre_low, preferred_element_type=jnp.float32)
    grad_mlp_in = jnp.dot(grad_pre_low, up_weight.T, preferred_element_type=jnp.float32)
    grad_dense = jnp.dot(attended_flat.T, cotangent, preferred_element_type=jnp.float32)
    grad_attended = jnp.dot(cotangent, dense_weight.T, preferred_element_type=jnp.float32)
    grad_attended = grad_attended.astype(jnp.bfloat16).reshape(TOKENS, H, HD)
    grad_att_float = grad_attended.astype(jnp.float32)
    delta_rows = lax.optimization_barrier(jnp.sum(grad_att_float * attended.astype(jnp.float32), axis=-1))

    def backward_step(carried, number):
        key_grad, value_grad = carried
        start_row, query_block, visible, scores = block_scores(number)
        grad_block = lax.dynamic_slice_in_dim(grad_att_float, start_row, block, 0)
        delta_block = lax.dynamic_slice_in_dim(delta_rows, start_row, block, 0)
        weights = jnp.where(visible[None], jnp.exp(scores - log_total[number][..., None]), 0.0)
        low = lax.optimization_barrier(weights.astype(jnp.bfloat16)).astype(jnp.float32)
        grad_weights = jnp.einsum('qhd,khd->hqk', grad_block, value_float)
        grad_scores = weights * (grad_weights - jnp.transpose(delta_block)[..., None])
        grad_low = lax.optimization_barrier(grad_scores.astype(jnp.bfloat16)).astype(jnp.float32)
        query_grad = jnp.einsum('hqk,khd->qhd', grad_low, key_float) * score_scale
        key_grad = key_grad + jnp.einsum('hqk,qhd->khd', grad_low, query_block) * score_scale
        value_grad = value_grad + jnp.einsum('hqk,qhd->khd', low, grad_block)
        return ((key_grad, value_grad), query_grad)
    zero_grads = (jnp.zeros((TOKENS, H, HD), jnp.float32), jnp.zeros((TOKENS, H, HD), jnp.float32))
    (key_grad, value_grad), query_grad = lax.scan(backward_step, zero_grads, jnp.arange(count))
    query_grad = query_grad.reshape(TOKENS, H, HD)
    grad_query_pre = rotate(query_grad, cosines, -sines)
    grad_key_pre = rotate(key_grad, cosines, -sines)
    grad_qv_bias = jnp.stack([lax.optimization_barrier(jnp.sum(grad_query_pre, axis=0)).reshape(width), lax.optimization_barrier(jnp.sum(value_grad, axis=0)).reshape(width)])
    grad_proj = jnp.stack([grad_query_pre, grad_key_pre, value_grad], axis=1)
    grad_proj = grad_proj.reshape(TOKENS, 3 * width).astype(jnp.bfloat16)
    grad_qkv = jnp.dot(attn_in.T, grad_proj, preferred_element_type=jnp.float32).reshape(D, 3, width)
    grad_attn_in = jnp.dot(grad_proj, qkv_weight.reshape(D, 3 * width).T, preferred_element_type=jnp.float32)
    grad_input = grad_out + norm_backward(grad_attn_in, hat_one, std_one, attn_scale)
    grad_input = grad_input + norm_backward(grad_mlp_in, hat_two, std_two, mlp_scale)
    grad_attn_scale = lax.optimization_barrier(jnp.sum(grad_attn_in * hat_one, axis=0))
    grad_attn_shift = lax.optimization_barrier(jnp.sum(grad_attn_in, axis=0))
    grad_mlp_scale = lax.optimization_barrier(jnp.sum(grad_mlp_in * hat_two, axis=0))
    grad_mlp_shift = lax.optimization_barrier(jnp.sum(grad_mlp_in, axis=0))
    return (output, grad_input, grad_attn_scale, grad_attn_shift, grad_mlp_scale, grad_mlp_shift, grad_qkv, grad_qv_bias, grad_dense, bias_grad, grad_up, grad_up_bias, grad_down, bias_grad)
```

```python
import jax
import jax.numpy as jnp
from jax import lax
from jax.experimental import pallas as pl
from jax.experimental.pallas import tpu as pltpu
from jax.sharding import PartitionSpec as P

D = 768
HD = 64
ROT = 16


norm_eps = 1e-05


def layer_norm(values, scale, shift):
    mean_value = jnp.mean(values, axis=-1, keepdims=True)
    centred = values - mean_value
    variance = jnp.mean(centred * centred, axis=-1, keepdims=True)
    inv_std = lax.rsqrt(variance + norm_eps)
    normal_part = centred * inv_std
    return (normal_part * scale + shift, normal_part, inv_std)


def norm_backward(grad_normed, normal_part, inv_std, scale):
    grad_hat = grad_normed * scale
    mean_grad = jnp.mean(grad_hat, axis=-1, keepdims=True)
    mean_mixed = jnp.mean(grad_hat * normal_part, axis=-1, keepdims=True)
    return inv_std * (grad_hat - mean_grad - normal_part * mean_mixed)


def rotary_tables(positions):
    freqs = 10000.0 ** (-jnp.arange(0, ROT, 2).astype(jnp.float32) / ROT)
    angles = positions.astype(jnp.float32)[:, None] * freqs[None, :]
    angles = jnp.concatenate([angles, angles], axis=1)
    return (jnp.cos(angles), jnp.sin(angles))


def rotate(tensor, cosines, sines):
    part = tensor[..., :ROT]
    half = ROT // 2
    turned = jnp.concatenate([-part[..., half:], part[..., :half]], axis=-1)
    spun = part * cosines + turned * sines
    return jnp.concatenate([spun, tensor[..., ROT:]], axis=-1)


def gelu_grad(pre_act):
    cumulative = 0.5 * (1.0 + jax.scipy.special.erf(pre_act * 0.7071067811865476))
    density = jnp.exp(-0.5 * pre_act * pre_act) * 0.3989422804014327
    return cumulative + pre_act * density


NEG = -1e30
CONTRACT_LAST = (((1,), (1,)), ((), ()))
CONTRACT_FIRST = (((0,), (0,)), ((), ()))


def attention_kernel(bounds, first_ref, q_ref, g_ref, kv_ref, att_ref, dq_ref, dkv_ref):
    low, own = bounds[0], bounds[1]
    rows = q_ref.shape[1]
    queries = q_ref[0]
    grads = g_ref[0]
    first_key = first_ref[...]
    query_pos = own * rows + lax.broadcasted_iota(jnp.int32, (rows, 1), 0)

    def masked_scores(j, block):
        scores = lax.dot_general(queries, block, CONTRACT_LAST, preferred_element_type=jnp.float32)
        key_pos = j * rows + lax.broadcasted_iota(jnp.int32, (1, rows), 1)
        visible = (key_pos <= query_pos) & (key_pos >= first_key)
        return jnp.where(visible, scores, NEG), visible

    def forward(j, state):
        row_max, row_sum, total = state
        block = kv_ref[j, 0]
        scores, visible = masked_scores(j, block)
        new_max = jnp.maximum(row_max, jnp.max(scores, axis=1, keepdims=True))
        weights = jnp.where(visible, jnp.exp(scores - new_max), 0.0)
        factor = jnp.exp(row_max - new_max)
        row_sum = row_sum * factor + jnp.sum(weights, axis=1, keepdims=True)
        total = total * factor + jnp.dot(
            weights.astype(jnp.bfloat16), block, preferred_element_type=jnp.float32
        )
        return new_max, row_sum, total

    row_max, row_sum, total = lax.fori_loop(
        low,
        own + 1,
        forward,
        (
            jnp.full((rows, 1), NEG, jnp.float32),
            jnp.zeros((rows, 1), jnp.float32),
            jnp.zeros((rows, 2 * HD), jnp.float32),
        ),
    )
    attended = (total / row_sum).astype(jnp.bfloat16)
    att_ref[0] = attended
    log_total = row_max + jnp.log(row_sum)
    delta = jnp.sum(
        grads.astype(jnp.float32) * attended.astype(jnp.float32), axis=1, keepdims=True
    )
    dkv_ref[...] = jnp.zeros_like(dkv_ref)

    def backward(j, query_grad):
        block = kv_ref[j, 0]
        scores, visible = masked_scores(j, block)
        weights = jnp.where(visible, jnp.exp(scores - log_total), 0.0)
        grad_weights = lax.dot_general(
            grads, block, CONTRACT_LAST, preferred_element_type=jnp.float32
        )
        grad_scores = (weights * (grad_weights - delta)).astype(jnp.bfloat16)
        dkv = lax.dot_general(
            grad_scores, queries, CONTRACT_FIRST, preferred_element_type=jnp.float32
        ) + lax.dot_general(
            weights.astype(jnp.bfloat16), grads, CONTRACT_FIRST, preferred_element_type=jnp.float32
        )
        dkv_ref[j, 0] = dkv.astype(jnp.bfloat16)
        return query_grad + jnp.dot(grad_scores, block, preferred_element_type=jnp.float32)

    dq_ref[0] = lax.fori_loop(low, own + 1, backward, jnp.zeros((rows, 2 * HD), jnp.float32))


def attention(bounds, first_key, queries, grads, key_values):
    heads, rows, lanes = queries.shape
    blocks = key_values.shape[0]
    per_head = pl.BlockSpec((1, rows, lanes), lambda h, b: (h, 0, 0))
    all_blocks = pl.BlockSpec((blocks, 1, rows, lanes), lambda h, b: (0, h, 0, 0))
    return pl.pallas_call(
        attention_kernel,
        grid_spec=pltpu.PrefetchScalarGridSpec(
            num_scalar_prefetch=1,
            grid=(heads,),
            in_specs=[
                pl.BlockSpec((rows, 1), lambda h, b: (0, 0)),
                per_head,
                per_head,
                all_blocks,
            ],
            out_specs=[per_head, per_head, all_blocks],
        ),
        out_shape=[
            jax.ShapeDtypeStruct(queries.shape, jnp.bfloat16),
            jax.ShapeDtypeStruct(queries.shape, jnp.float32),
            jax.ShapeDtypeStruct(key_values.shape, jnp.bfloat16),
        ],
        cost_estimate=pl.CostEstimate(
            flops=14 * heads * rows * rows * blocks * lanes,
            bytes_accessed=4 * heads * rows * blocks * lanes,
            transcendentals=2 * heads * rows * rows * blocks,
        ),
    )(bounds, first_key, queries, grads, key_values)


def local(
    inputs,
    positions,
    attn_scale,
    attn_shift,
    mlp_scale,
    mlp_shift,
    qkv_weight,
    qv_bias,
    dense_weight,
    dense_bias,
    up_weight,
    up_bias,
    down_weight,
    down_bias,
    cotangent,
):
    f32, bf16 = jnp.float32, jnp.bfloat16
    local_width = qkv_weight.shape[2]
    hidden = up_weight.shape[1]
    heads = local_width // HD
    score_scale = HD ** (-0.5)
    own_rows = inputs.shape[0]
    tp_index = lax.axis_index("tp")
    ctx_index = lax.axis_index("ctx")
    both = lax.all_gather(
        jnp.concatenate([inputs, cotangent], axis=1), "tp", axis=0, tiled=True
    )
    rows = both.shape[0]
    grad_full = both[:, D:]
    normed_one, hat_one, std_one = layer_norm(both[:, :D].astype(f32), attn_scale, attn_shift)
    normed_two = hat_one * mlp_scale + mlp_shift
    attn_in = normed_one.astype(bf16)
    mlp_in = normed_two.astype(bf16)
    proj = jnp.dot(
        attn_in, qkv_weight.reshape(D, 3 * local_width), preferred_element_type=f32
    )
    proj = jnp.transpose(proj.reshape(rows, 3, heads, HD), (1, 2, 0, 3))
    cosines, sines = rotary_tables(positions)
    biases = qv_bias.reshape(2, heads, 1, HD)
    queries = rotate(proj[0] + biases[0], cosines, sines).astype(bf16) * bf16(score_scale)
    keys_rot = rotate(proj[1], cosines, sines).astype(bf16)
    values = (proj[2] + biases[1]).astype(bf16)
    own_kv = jnp.concatenate([keys_rot, values], axis=2)
    key_values = lax.all_gather(own_kv, "ctx", axis=0, tiled=False)

    grad_attended = jnp.dot(grad_full, dense_weight.T, preferred_element_type=f32).astype(bf16)
    grad_attended = jnp.transpose(grad_attended.reshape(rows, heads, HD), (1, 0, 2))
    blank = jnp.zeros((heads, rows, HD), bf16)
    padded_queries = jnp.concatenate([queries, blank], axis=2)
    padded_grads = jnp.concatenate([blank, grad_attended], axis=2)
    first_key = ctx_index * rows + jnp.arange(rows, dtype=jnp.int32) - positions
    bounds = jnp.stack([jnp.min(first_key) // rows, ctx_index]).astype(jnp.int32)

    pre_act = jnp.dot(mlp_in, up_weight, preferred_element_type=f32) + up_bias
    activation = jax.nn.gelu(pre_act, approximate=False).astype(bf16)
    mlp_part = jnp.dot(activation, down_weight, preferred_element_type=f32)
    grad_down = jnp.dot(activation.T, grad_full, preferred_element_type=f32)
    grad_act = jnp.dot(grad_full, down_weight.T, preferred_element_type=f32)
    grad_pre = grad_act * gelu_grad(pre_act)
    grad_up_bias = jnp.sum(grad_pre, axis=0)
    grad_pre_low = grad_pre.astype(bf16)
    grad_up = jnp.dot(mlp_in.T, grad_pre_low, preferred_element_type=f32)
    grad_mlp_in = jnp.dot(grad_pre_low, up_weight.T, preferred_element_type=f32)
    early = jnp.concatenate(
        [grad_up.astype(bf16).reshape(-1, D), grad_down.astype(bf16)], axis=0
    )
    early_low = lax.psum(early, "ctx")

    attended, query_grad, key_terms = attention(
        bounds, first_key[:, None], padded_queries, padded_grads, key_values
    )
    own_terms = lax.psum_scatter(key_terms, "ctx", scatter_dimension=0, tiled=True)[0]
    own_terms = own_terms.astype(f32)
    attended_flat = jnp.transpose(attended[:, :, HD:], (1, 0, 2)).reshape(rows, local_width)
    attn_part = jnp.dot(attended_flat, dense_weight, preferred_element_type=f32)
    grad_dense = jnp.dot(attended_flat.T, grad_full, preferred_element_type=f32)
    own_sums = lax.psum_scatter(
        jnp.concatenate([(attn_part + mlp_part).astype(bf16), grad_mlp_in.astype(bf16)], axis=1),
        "tp",
        scatter_dimension=0,
        tiled=True,
    ).astype(f32)
    branch_sum, own_mlp = own_sums[:, :D], own_sums[:, D:]
    resid = inputs.astype(f32)
    output = (resid + branch_sum + dense_bias + down_bias).astype(bf16)

    grad_query_pre = rotate(query_grad[:, :, :HD] * score_scale, cosines, -sines)
    grad_key_pre = rotate(own_terms[:, :, :HD], cosines, -sines)
    value_grad = own_terms[:, :, HD:]
    grad_proj = jnp.stack([grad_query_pre, grad_key_pre, value_grad]).astype(bf16)
    grad_proj = jnp.transpose(grad_proj, (2, 0, 1, 3)).reshape(rows, 3 * local_width)
    grad_attn_in = jnp.dot(
        grad_proj, qkv_weight.reshape(D, 3 * local_width).T, preferred_element_type=f32
    )
    own_attn = lax.psum_scatter(
        grad_attn_in.astype(bf16), "tp", scatter_dimension=0, tiled=True
    ).astype(f32)
    grad_qkv = jnp.dot(attn_in.T, grad_proj, preferred_element_type=f32)
    late = jnp.concatenate(
        [grad_qkv.astype(bf16).reshape(-1, D), grad_dense.astype(bf16)], axis=0
    )
    late, early_low = lax.optimization_barrier((late, early_low))
    early_sum = early_low.astype(f32)
    late_sum = lax.psum(late, "ctx").astype(f32)

    grad_out = cotangent.astype(f32)
    small = jnp.concatenate(
        [
            jnp.sum(grad_attn_in * hat_one, axis=0),
            jnp.sum(grad_attn_in, axis=0),
            jnp.sum(grad_mlp_in * hat_one, axis=0),
            jnp.sum(grad_mlp_in, axis=0),
            jnp.sum(grad_out, axis=0),
            jnp.sum(grad_query_pre, axis=1).reshape(-1),
            jnp.sum(value_grad, axis=1).reshape(-1),
            grad_up_bias,
        ]
    )
    gathered = lax.all_gather(small[None], ("ctx", "tp"), axis=0, tiled=True)
    shared = jnp.sum(gathered[:, : 5 * D], axis=0).reshape(5, D)
    per_tp = jnp.sum(gathered[:, 5 * D :].reshape(-1, lax.axis_size("tp"), 2 * local_width + hidden), axis=0)
    mine = lax.dynamic_index_in_dim(per_tp, tp_index, 0, keepdims=False)

    hat = lax.dynamic_slice_in_dim(hat_one, tp_index * own_rows, own_rows, 0)
    std = lax.dynamic_slice_in_dim(std_one, tp_index * own_rows, own_rows, 0)
    grad_input = grad_out + norm_backward(own_attn, hat, std, attn_scale)
    grad_input = grad_input + norm_backward(own_mlp, hat, std, mlp_scale)
    qkv_rows = late_sum.shape[0] - local_width
    up_rows = early_sum.shape[0] - hidden
    return (
        output,
        grad_input,
        shared[0],
        shared[1],
        shared[2],
        shared[3],
        late_sum[:qkv_rows].reshape(D, 3, local_width),
        mine[: 2 * local_width].reshape(2, local_width),
        late_sum[qkv_rows:],
        shared[4],
        early_sum[:up_rows].reshape(D, hidden),
        mine[2 * local_width :],
        early_sum[up_rows:],
        shared[4],
    )


def solution(mesh):
    in_specs = (
        P(("ctx", "tp"), None),
        P("ctx"),
        P(),
        P(),
        P(),
        P(),
        P(None, None, "tp"),
        P(None, "tp"),
        P("tp", None),
        P(),
        P(None, "tp"),
        P("tp"),
        P("tp", None),
        P(),
        P(("ctx", "tp"), None),
    )
    out_specs = (
        P(("ctx", "tp"), None),
        P(("ctx", "tp"), None),
        P(),
        P(),
        P(),
        P(),
        P(None, None, "tp"),
        P(None, "tp"),
        P("tp", None),
        P(),
        P(None, "tp"),
        P("tp"),
        P("tp", None),
        P(),
    )
    return jax.shard_map(local, mesh=mesh, in_specs=in_specs, out_specs=out_specs, check_vma=False)
```

```python
import jax
import jax.numpy as jnp
from jax import lax
from jax.experimental import pallas as pl
from jax.experimental.pallas import tpu as pltpu
from jax.sharding import PartitionSpec as P

D = 768
HD = 64
ROT = 16


norm_eps = 1e-05


def layer_norm(values, scale, shift):
    mean_value = jnp.mean(values, axis=-1, keepdims=True)
    centred = values - mean_value
    variance = jnp.mean(centred * centred, axis=-1, keepdims=True)
    inv_std = lax.rsqrt(variance + norm_eps)
    normal_part = centred * inv_std
    return (normal_part * scale + shift, normal_part, inv_std)


def norm_backward(grad_normed, normal_part, inv_std, scale):
    grad_hat = grad_normed * scale
    mean_grad = jnp.mean(grad_hat, axis=-1, keepdims=True)
    mean_mixed = jnp.mean(grad_hat * normal_part, axis=-1, keepdims=True)
    return inv_std * (grad_hat - mean_grad - normal_part * mean_mixed)


def rotary_tables(positions):
    freqs = 10000.0 ** (-jnp.arange(0, ROT, 2).astype(jnp.float32) / ROT)
    angles = positions.astype(jnp.float32)[:, None] * jnp.tile(freqs, HD // (ROT // 2))[None, :]
    spun = (jnp.arange(HD) < ROT)[None, :]
    return (jnp.where(spun, jnp.cos(angles), 1.0), jnp.where(spun, jnp.sin(angles), 0.0))


def rotate(tensor, cosines, sines):
    half = ROT // 2
    source, target = jnp.arange(HD)[:, None], jnp.arange(HD)[None, :]
    swap = jnp.where((target < half) & (source == target + half), -1.0, 0.0)
    swap += jnp.where((target >= half) & (target < ROT) & (source == target - half), 1.0, 0.0)
    turned = jnp.dot(tensor, swap, precision=lax.Precision.HIGHEST)
    return tensor * cosines + turned * sines


def gelu_grad(pre_act):
    cumulative = 0.5 * (1.0 + jax.scipy.special.erf(pre_act * 0.7071067811865476))
    density = jnp.exp(-0.5 * pre_act * pre_act) * 0.3989422804014327
    return cumulative + pre_act * density


NEG = -1e30
CONTRACT_LAST = (((1,), (1,)), ((), ()))
CONTRACT_FIRST = (((0,), (0,)), ((), ()))


def attention_kernel(bounds, first_ref, q_ref, g_ref, kv_ref, att_ref, dq_ref, dkv_ref):
    low, own = bounds[0], bounds[1]
    rows = q_ref.shape[1]
    queries = q_ref[0]
    grads = g_ref[0]
    first_key = first_ref[...]
    query_pos = own * rows + lax.broadcasted_iota(jnp.int32, (rows, 1), 0)

    def masked_scores(j, block):
        scores = lax.dot_general(queries, block, CONTRACT_LAST, preferred_element_type=jnp.float32)
        key_pos = j * rows + lax.broadcasted_iota(jnp.int32, (1, rows), 1)
        visible = (key_pos <= query_pos) & (key_pos >= first_key)
        return jnp.where(visible, scores, NEG), visible

    def forward(j, state):
        row_max, row_sum, total = state
        block = kv_ref[j, 0]
        scores, visible = masked_scores(j, block)
        new_max = jnp.maximum(row_max, jnp.max(scores, axis=1, keepdims=True))
        weights = jnp.where(visible, jnp.exp(scores - new_max), 0.0)
        factor = jnp.exp(row_max - new_max)
        row_sum = row_sum * factor + jnp.sum(weights, axis=1, keepdims=True)
        total = total * factor + jnp.dot(
            weights.astype(jnp.bfloat16), block, preferred_element_type=jnp.float32
        )
        return new_max, row_sum, total

    row_max, row_sum, total = lax.fori_loop(
        low,
        own + 1,
        forward,
        (
            jnp.full((rows, 1), NEG, jnp.float32),
            jnp.zeros((rows, 1), jnp.float32),
            jnp.zeros((rows, 2 * HD), jnp.float32),
        ),
    )
    attended = (total / row_sum).astype(jnp.bfloat16)
    att_ref[0] = attended
    log_total = row_max + jnp.log(row_sum)
    delta = jnp.sum(
        grads.astype(jnp.float32) * attended.astype(jnp.float32), axis=1, keepdims=True
    )
    dkv_ref[...] = jnp.zeros_like(dkv_ref)

    def backward(j, query_grad):
        block = kv_ref[j, 0]
        scores, visible = masked_scores(j, block)
        weights = jnp.where(visible, jnp.exp(scores - log_total), 0.0)
        grad_weights = lax.dot_general(
            grads, block, CONTRACT_LAST, preferred_element_type=jnp.float32
        )
        grad_scores = (weights * (grad_weights - delta)).astype(jnp.bfloat16)
        dkv = lax.dot_general(
            grad_scores, queries, CONTRACT_FIRST, preferred_element_type=jnp.float32
        ) + lax.dot_general(
            weights.astype(jnp.bfloat16), grads, CONTRACT_FIRST, preferred_element_type=jnp.float32
        )
        dkv_ref[j, 0] = dkv.astype(jnp.bfloat16)
        return query_grad + jnp.dot(grad_scores, block, preferred_element_type=jnp.float32)

    dq_ref[0] = lax.fori_loop(low, own + 1, backward, jnp.zeros((rows, 2 * HD), jnp.float32))


def attention(bounds, first_key, queries, grads, key_values):
    heads, rows, lanes = queries.shape
    blocks = key_values.shape[0]
    per_head = pl.BlockSpec((1, rows, lanes), lambda h, b: (h, 0, 0))
    all_blocks = pl.BlockSpec((blocks, 1, rows, lanes), lambda h, b: (0, h, 0, 0))
    return pl.pallas_call(
        attention_kernel,
        grid_spec=pltpu.PrefetchScalarGridSpec(
            num_scalar_prefetch=1,
            grid=(heads,),
            in_specs=[
                pl.BlockSpec((rows, 1), lambda h, b: (0, 0)),
                per_head,
                per_head,
                all_blocks,
            ],
            out_specs=[per_head, per_head, all_blocks],
        ),
        out_shape=[
            jax.ShapeDtypeStruct(queries.shape, jnp.bfloat16),
            jax.ShapeDtypeStruct(queries.shape, jnp.float32),
            jax.ShapeDtypeStruct(key_values.shape, jnp.bfloat16),
        ],
        cost_estimate=pl.CostEstimate(
            flops=14 * heads * rows * rows * blocks * lanes,
            bytes_accessed=4 * heads * rows * blocks * lanes,
            transcendentals=2 * heads * rows * rows * blocks,
        ),
    )(bounds, first_key, queries, grads, key_values)


def local(
    inputs,
    positions,
    attn_scale,
    attn_shift,
    mlp_scale,
    mlp_shift,
    qkv_weight,
    qv_bias,
    dense_weight,
    dense_bias,
    up_weight,
    up_bias,
    down_weight,
    down_bias,
    cotangent,
):
    f32, bf16 = jnp.float32, jnp.bfloat16
    local_width = qkv_weight.shape[2]
    hidden = up_weight.shape[1]
    heads = local_width // HD
    score_scale = HD ** (-0.5)
    own_rows = inputs.shape[0]
    tp_index = lax.axis_index("tp")
    ctx_index = lax.axis_index("ctx")
    both = lax.all_gather(
        jnp.concatenate([inputs, cotangent], axis=1), "tp", axis=0, tiled=True
    )
    rows = both.shape[0]
    grad_full = both[:, D:]
    normed_one, hat_one, std_one = layer_norm(both[:, :D].astype(f32), attn_scale, attn_shift)
    normed_two = hat_one * mlp_scale + mlp_shift
    attn_in = normed_one.astype(bf16)
    mlp_in = normed_two.astype(bf16)
    proj = jnp.dot(
        attn_in, qkv_weight.reshape(D, 3 * local_width), preferred_element_type=f32
    )
    proj = jnp.transpose(proj.reshape(rows, 3, heads, HD), (1, 2, 0, 3))
    cosines, sines = rotary_tables(positions)
    biases = qv_bias.reshape(2, heads, 1, HD)
    queries = rotate(proj[0] + biases[0], cosines, sines).astype(bf16) * bf16(score_scale)
    keys_rot = rotate(proj[1], cosines, sines).astype(bf16)
    values = (proj[2] + biases[1]).astype(bf16)
    own_kv = jnp.concatenate([keys_rot, values], axis=2)
    key_values = lax.all_gather(own_kv, "ctx", axis=0, tiled=False)

    grad_attended = jnp.dot(grad_full, dense_weight.T, preferred_element_type=f32).astype(bf16)
    grad_attended = jnp.transpose(grad_attended.reshape(rows, heads, HD), (1, 0, 2))
    blank = jnp.zeros((heads, rows, HD), bf16)
    padded_queries = jnp.concatenate([queries, blank], axis=2)
    padded_grads = jnp.concatenate([blank, grad_attended], axis=2)
    first_key = ctx_index * rows + jnp.arange(rows, dtype=jnp.int32) - positions
    bounds = jnp.stack([jnp.min(first_key) // rows, ctx_index]).astype(jnp.int32)

    pre_act = jnp.dot(mlp_in, up_weight, preferred_element_type=f32) + up_bias
    activation = jax.nn.gelu(pre_act, approximate=False).astype(bf16)
    mlp_part = jnp.dot(activation, down_weight, preferred_element_type=f32)
    grad_down = jnp.dot(activation.T, grad_full, preferred_element_type=f32)
    grad_act = jnp.dot(grad_full, down_weight.T, preferred_element_type=f32)
    grad_pre = grad_act * gelu_grad(pre_act)
    grad_up_bias = jnp.sum(grad_pre, axis=0)
    grad_pre_low = grad_pre.astype(bf16)
    grad_up = jnp.dot(mlp_in.T, grad_pre_low, preferred_element_type=f32)
    grad_mlp_in = jnp.dot(grad_pre_low, up_weight.T, preferred_element_type=f32)
    early = jnp.concatenate(
        [grad_up.astype(bf16).reshape(-1, D), grad_down.astype(bf16)], axis=0
    )
    key_values, early = lax.optimization_barrier((key_values, early))
    early_low = lax.psum(early, "ctx")

    attended, query_grad, key_terms = attention(
        bounds, first_key[:, None], padded_queries, padded_grads, key_values
    )
    key_terms, early_low = lax.optimization_barrier((key_terms, early_low))
    own_terms = lax.psum_scatter(key_terms, "ctx", scatter_dimension=0, tiled=True)[0]
    own_terms = own_terms.astype(f32)
    attended_flat = jnp.transpose(attended[:, :, HD:], (1, 0, 2)).reshape(rows, local_width)
    attn_part = jnp.dot(attended_flat, dense_weight, preferred_element_type=f32)
    grad_dense = jnp.dot(attended_flat.T, grad_full, preferred_element_type=f32)
    grad_query_pre = rotate(query_grad[:, :, :HD] * score_scale, cosines, -sines)
    grad_key_pre = rotate(own_terms[:, :, :HD], cosines, -sines)
    value_grad = own_terms[:, :, HD:]
    grad_proj = jnp.stack([grad_query_pre, grad_key_pre, value_grad]).astype(bf16)
    grad_proj = jnp.transpose(grad_proj, (2, 0, 1, 3)).reshape(rows, 3 * local_width)
    grad_attn_in = jnp.dot(
        grad_proj, qkv_weight.reshape(D, 3 * local_width).T, preferred_element_type=f32
    )
    grad_qkv = jnp.dot(attn_in.T, grad_proj, preferred_element_type=f32)
    late = jnp.concatenate(
        [grad_qkv.astype(bf16).reshape(-1, D), grad_dense.astype(bf16)], axis=0
    )
    grad_out = cotangent.astype(f32)
    small = jnp.concatenate(
        [
            jnp.sum(grad_attn_in * hat_one, axis=0),
            jnp.sum(grad_attn_in, axis=0),
            jnp.sum(grad_mlp_in * hat_one, axis=0),
            jnp.sum(grad_mlp_in, axis=0),
            jnp.sum(grad_out, axis=0),
            jnp.sum(grad_query_pre, axis=1).reshape(-1),
            jnp.sum(value_grad, axis=1).reshape(-1),
            grad_up_bias,
        ]
    )
    late, small = lax.optimization_barrier((late, small))
    gathered = lax.all_gather(small[None], ("ctx", "tp"), axis=0, tiled=True)
    branches = jnp.concatenate(
        [part.astype(bf16) for part in (attn_part + mlp_part, grad_mlp_in, grad_attn_in)], axis=1
    )
    branches, gathered = lax.optimization_barrier((branches, gathered))
    own_sums = lax.psum_scatter(branches, "tp", scatter_dimension=0, tiled=True).astype(f32)
    branch_sum, own_mlp, own_attn = jnp.split(own_sums, 3, axis=1)
    resid = inputs.astype(f32)
    output = (resid + branch_sum + dense_bias + down_bias).astype(bf16)
    early_sum = early_low.astype(f32)
    late_sum = lax.psum(late, "ctx").astype(f32)
    shared = jnp.sum(gathered[:, : 5 * D], axis=0).reshape(5, D)
    per_tp = jnp.sum(gathered[:, 5 * D :].reshape(-1, lax.axis_size("tp"), 2 * local_width + hidden), axis=0)
    mine = lax.dynamic_index_in_dim(per_tp, tp_index, 0, keepdims=False)

    hat = lax.dynamic_slice_in_dim(hat_one, tp_index * own_rows, own_rows, 0)
    std = lax.dynamic_slice_in_dim(std_one, tp_index * own_rows, own_rows, 0)
    grad_input = grad_out + norm_backward(own_attn, hat, std, attn_scale)
    grad_input = grad_input + norm_backward(own_mlp, hat, std, mlp_scale)
    qkv_rows = late_sum.shape[0] - local_width
    up_rows = early_sum.shape[0] - hidden
    return (
        output,
        grad_input,
        shared[0],
        shared[1],
        shared[2],
        shared[3],
        late_sum[:qkv_rows].reshape(D, 3, local_width),
        mine[: 2 * local_width].reshape(2, local_width),
        late_sum[qkv_rows:],
        shared[4],
        early_sum[:up_rows].reshape(D, hidden),
        mine[2 * local_width :],
        early_sum[up_rows:],
        shared[4],
    )


def solution(mesh):
    in_specs = (
        P(("ctx", "tp"), None),
        P("ctx"),
        P(),
        P(),
        P(),
        P(),
        P(None, None, "tp"),
        P(None, "tp"),
        P("tp", None),
        P(),
        P(None, "tp"),
        P("tp"),
        P("tp", None),
        P(),
        P(("ctx", "tp"), None),
    )
    out_specs = (
        P(("ctx", "tp"), None),
        P(("ctx", "tp"), None),
        P(),
        P(),
        P(),
        P(),
        P(None, None, "tp"),
        P(None, "tp"),
        P("tp", None),
        P(),
        P(None, "tp"),
        P("tp"),
        P("tp", None),
        P(),
    )
    return jax.shard_map(local, mesh=mesh, in_specs=in_specs, out_specs=out_specs, check_vma=False)
```
